512 devices in a mesh: dp: 16 (over y, z_hi, core), expert: 32 (over z_lo, x).
Axes of the slice: x: 4, y: 4, z: 16 (z_hi: 2, z_lo: 8; z = z_hi * 8 + z_lo), core: 2. Of those that a mesh axis runs over, the one named last changes fastest.
Arguments:
- tokens: bfloat16 [1536, 3584], P('dp', 'expert'), may hold values from -13 to 13
- routes: int32 [1536, 8], replicated, may hold values from 0 to 31, all different within a row; in each aligned block of 96 rows (0 to 95, 96 to 191, ...) at most 32 rows name the same one
- gate_weight: bfloat16 [32, 3584, 2048], P('expert', None, 'dp'), may hold values from -0.09375 to 0.09375
- up_weight: bfloat16 [32, 3584, 2048], P('expert', None, 'dp'), may hold values from -0.09375 to 0.09375
- hidden_grad: bfloat16 [32, 16, 32, 2048], P('expert', None, None, 'dp'), may hold values from -40 to 40
- clip_limit: float32 [32], P('expert'), may hold values from 1 to 40
Outputs:
- hidden: bfloat16 [32, 16, 32, 2048], P('expert', None, None, 'dp')
- grad_gate: bfloat16 [32, 3584, 2048], P('expert', None, 'dp')
- grad_up: bfloat16 [32, 3584, 2048], P('expert', None, 'dp')
- token_grad: bfloat16 [1536, 3584], P('dp', 'expert')
The draws below stay inside these ranges and needn't reach their ends.
Inputs may be any that keep to these rules, and one draw needn't show every extreme that they name: `routes`: each row names 8 different experts. In each aligned block of 96 rows (the tokens of one index of dp) no expert is named by more than 32 rows, a bound that some block reaches.
All inputs are finite; a program needn't handle non-finite values.
Results may differ from the reference program's by a relative error of at most 0.014.
Values may be sent and summed in bfloat16 or wider, within the bound.
No kernel may reach another device: no remote copies, remote signals or barrier semaphores. Data moves between devices by JAX's collectives and lax.ppermute only.
A program may use at most 64 MiB of HBM per device.

```python
import math
import jax
import jax.numpy as jnp
import numpy as np
from jax import lax

D = 3584
F = 2048
TOP = 8
EXPERTS = 32
CAP = 32
TOK_DEV = 96
TOKENS = 1536
HID = 128
N_DP = 16


def draw_tokens(key, part):
    key_values, key_scale = jax.random.split(key, 2)
    column_scale = 10.0 ** (jax.random.uniform(key_scale, (1, D), jnp.float32) - 0.5)
    values = jax.random.truncated_normal(key_values, -4.0, 4.0, (TOKENS, D), jnp.float32)
    return (values * column_scale).astype(jnp.bfloat16)


def draw_hidden_grad(key, part):
    key_values, key_columns, key_rows = jax.random.split(key, 3)
    unit_pos = (jnp.arange(F, dtype=jnp.float32) + 0.5) / F
    column_scale = 10.0 ** (jax.random.uniform(key_columns, (F,), jnp.float32) - 0.75) * 3.0 ** (unit_pos - 0.5)
    row_scale = 10.0 ** (jax.random.uniform(key_rows, (EXPERTS, N_DP, CAP, 1), jnp.float32) - 0.5)
    values = jax.random.truncated_normal(key_values, -4.0, 4.0, (EXPERTS, N_DP, CAP, F), jnp.float32)
    return (values * column_scale * row_scale).astype(jnp.bfloat16)


def levels(rng, shape, pieces, low, top_value):
    def one(dim, shards_of):
        steps = jax.random.uniform(jax.random.fold_in(jax.random.fold_in(rng, 6), dim), (shards_of,), jnp.float32, low / len(pieces), top_value / len(pieces))
        return jnp.repeat(jnp.exp(steps), shape[dim] // shards_of).reshape((-1,) + (1,) * (len(shape) - dim - 1))

    factor_of = one(*pieces[0])
    for cut in pieces[1:]:
        factor_of = factor_of * one(*cut)
    return factor_of


def assign_block(stream_key, own, number, rows, amount, top, bound, lean):
    order = jax.random.permutation(stream_key, amount)
    crowded, usual = load_shares(amount, rows * top, bound, lean, True), load_shares(amount, rows * top, bound, lean, False)
    places = jnp.arange(amount)

    def named(lengths, rotation):
        used = int((lengths > 0).sum())
        fixed = max(1, used // 4)
        shifted = fixed + (places - fixed + rotation * (used - fixed)) % max(1, amount - fixed)
        return jnp.zeros((amount,), jnp.int32).at[order[jnp.where(places < fixed, places, shifted)]].set(jnp.asarray(lengths, jnp.int32))

    lengths = jnp.where(number % 4 == 0, named(crowded, number // 4), named(usual, number - number // 4 - 1))
    mixed = jax.random.permutation(jax.random.fold_in(own, 3), amount)
    source_of, receiver = mixed[0:amount // 2 * 2:2], mixed[1:amount // 2 * 2:2]
    margin = jnp.minimum(lengths[source_of] - 1, bound - lengths[receiver]) // 2
    margin = jnp.where((source_of == order[0]) | (receiver == order[0]) | (lengths[receiver] == 0), 0, jnp.maximum(margin, 0))
    shifted = jax.random.randint(jax.random.fold_in(own, 4), (amount // 2,), 0, 1 << 20) % (margin + 1)
    lengths = lengths.at[source_of].add(-shifted).at[receiver].add(shifted)
    members = jnp.searchsorted(jnp.cumsum(lengths), jnp.arange(rows * top), side="right").astype(jnp.int32)
    grid = members.reshape(top, rows).T
    grid = grid[jax.random.permutation(jax.random.fold_in(own, 1), rows)]
    rotation = jax.random.randint(jax.random.fold_in(own, 2), (rows, 1), 0, top)
    return jnp.take_along_axis(grid, (jnp.arange(top)[None, :] + rotation) % top, axis=1)


def load_shares(count, total, most, skew, full):
    portions = [(1 << 20) // math.isqrt(rank ** skew) + 1 for rank in range(1, count + 1)]
    largest = most if full else min(most, max(-(-total // count), total * portions[0] // sum(portions)))
    least = 1 if total - largest >= count - 1 else 0
    counts, spare = [largest] + [least] * (count - 1), total - largest - least * (count - 1)
    while spare > 0:
        free = [i for i in range(1, count) if counts[i] < largest] or [i for i in range(1, count) if counts[i] < most]
        pool, remaining = sum([portions[i] for i in free]), spare
        for i in free:
            addition = min(most - counts[i], max(1, remaining * portions[i] // pool), spare)
            counts[i] = counts[i] + addition
            spare = spare - addition
    return np.array(counts)


def bell_draw(own_key, dims, width, bound, pieces=(), kind=jnp.bfloat16):
    result = jax.random.normal(own_key, dims, jnp.float32) * width
    if len(pieces) > 0:
        result = levels(own_key, dims, pieces, -0.22, 0.18) * result
    return jnp.clip(result, min=-bound, max=bound).astype(kind)


def setup_inputs(seed: int = 0) -> dict:
    arg_keys = jax.random.split(jax.random.key(seed), 7)
    tokens = draw_tokens(jax.random.fold_in(arg_keys[6], 71), 0)
    routes_keys = jax.random.split(jax.random.fold_in(arg_keys[1], 1), TOKENS // TOK_DEV)
    routes_turns = jax.random.permutation(jax.random.fold_in(arg_keys[1], 3), TOKENS // TOK_DEV)
    routes = jax.vmap(lambda own, number: assign_block(jax.random.fold_in(arg_keys[1], 2), own, number, TOK_DEV, EXPERTS, TOP, CAP, 1))(routes_keys, routes_turns).reshape((TOKENS, TOP))
    gate_weight = bell_draw(arg_keys[2], (EXPERTS, D, F), D ** -0.5, 0.09375, ((0, 32), (2, 16)))
    up_weight = bell_draw(arg_keys[3], (EXPERTS, D, F), D ** -0.5, 0.09375, ((0, 32), (2, 16)))
    hidden_grad = draw_hidden_grad(jax.random.fold_in(arg_keys[6], 71), 0)
    clip_limit = jnp.clip(jnp.exp(math.log(40.0) - 3.6888795 * jax.random.uniform(arg_keys[5], (EXPERTS,), jnp.float32) ** levels(arg_keys[5], (EXPERTS,), ((0, 32),), -0.2, 0.2)), 1.0, 40.0)
    return dict(tokens=tokens, routes=routes, gate_weight=gate_weight, up_weight=up_weight, hidden_grad=hidden_grad, clip_limit=clip_limit)


def slot_tables(block_routes):
    flat_routes = block_routes.reshape(-1)
    expert_ids = jnp.arange(EXPERTS, dtype=jnp.int32)
    onehot = (flat_routes[:, None] == expert_ids[None, :]).astype(jnp.int32)
    before = jnp.cumsum(onehot, axis=0) - onehot
    slot_ranks = lax.optimization_barrier(jnp.sum(before * onehot, axis=1)).astype(jnp.int32)
    owner_token = (jnp.arange(flat_routes.shape[0], dtype=jnp.int32) // TOP).astype(jnp.int32)
    token_of = jnp.zeros((EXPERTS, CAP), jnp.int32).at[flat_routes, slot_ranks].set(owner_token)
    occupied = jnp.zeros((EXPERTS, CAP), jnp.bool_).at[flat_routes, slot_ranks].set(True)
    return (slot_ranks.reshape(block_routes.shape), token_of, occupied)

def expert_pass(packed_item):
    dispatched, gate_w, up_w, grad_hidden, limit = packed_item
    gate_pre = jnp.dot(dispatched, gate_w, preferred_element_type=jnp.float32)
    up_pre = jnp.dot(dispatched, up_w, preferred_element_type=jnp.float32)
    sigma_gate = jax.nn.sigmoid(gate_pre)
    hidden = (gate_pre * sigma_gate * up_pre).astype(jnp.bfloat16)
    grad_float = grad_hidden.astype(jnp.float32)
    up_act = (grad_float * gate_pre * sigma_gate).astype(jnp.bfloat16)
    gate_act = (grad_float * up_pre * sigma_gate * (1.0 + gate_pre * (1.0 - sigma_gate))).astype(jnp.bfloat16)
    raw_gate = jnp.dot(dispatched.T, gate_act, preferred_element_type=jnp.float32)
    raw_up = jnp.dot(dispatched.T, up_act, preferred_element_type=jnp.float32)
    norm_sq = jnp.sum(raw_gate * raw_gate) + jnp.sum(raw_up * raw_up)
    root_mean = jnp.sqrt(norm_sq / (2.0 * D * F) + 1e-06)
    clip_scale = jnp.minimum(1.0, limit / root_mean)
    row_count = dispatched.shape[0]
    gate_blocks = gate_act.astype(jnp.float32).reshape(row_count, N_DP, HID)
    up_blocks = up_act.astype(jnp.float32).reshape(row_count, N_DP, HID)
    weight_gate = gate_w.astype(jnp.float32).reshape(D, N_DP, HID)
    weight_up = up_w.astype(jnp.float32).reshape(D, N_DP, HID)
    partial_value = jnp.einsum('rbh,dbh->rbd', gate_blocks, weight_gate, precision=lax.Precision.HIGHEST)
    partial_value = partial_value + jnp.einsum('rbh,dbh->rbd', up_blocks, weight_up, precision=lax.Precision.HIGHEST)
    partial_value = lax.optimization_barrier(partial_value.astype(jnp.bfloat16))
    slot_grad = lax.optimization_barrier(jnp.sum(partial_value.astype(jnp.float32), axis=1))
    grad_gate = (clip_scale * raw_gate).astype(jnp.bfloat16)
    grad_up = (clip_scale * raw_up).astype(jnp.bfloat16)
    return (hidden, grad_gate, grad_up, slot_grad)

def reference(tokens, routes, gate_weight, up_weight, hidden_grad, clip_limit):
    blocks = routes.reshape(N_DP, TOK_DEV, TOP)
    slot_ranks, token_of, occupied = jax.vmap(slot_tables)(blocks)
    offsets = (jnp.arange(N_DP, dtype=jnp.int32) * TOK_DEV)[:, None, None]
    gathered = jnp.where(occupied[..., None], tokens[(token_of + offsets).astype(jnp.int32)], jnp.zeros((), tokens.dtype))
    gathered = jnp.transpose(gathered, (1, 0, 2, 3)).reshape(EXPERTS, N_DP * CAP, D)
    grads_in = hidden_grad.reshape(EXPERTS, N_DP * CAP, F)
    hidden, grad_gate, grad_up, slot_grad = lax.map(expert_pass, (gathered, gate_weight, up_weight, grads_in, clip_limit))
    flat_slots = slot_grad.reshape(EXPERTS * N_DP * CAP, D)
    dp_ids = jnp.arange(N_DP, dtype=jnp.int32)[:, None, None]
    positions = ((blocks * N_DP + dp_ids) * CAP + slot_ranks).astype(jnp.int32)
    token_grad = lax.optimization_barrier(jnp.sum(flat_slots[positions], axis=2)).reshape(TOKENS, D).astype(jnp.bfloat16)
    return (hidden.reshape(EXPERTS, N_DP, CAP, F), grad_gate, grad_up, token_grad)
```

```python
import jax
import jax.numpy as jnp
from jax import lax
from jax.sharding import Mesh, PartitionSpec as P


BF = jnp.bfloat16
F32 = jnp.float32


def shift(value, axis, step):
    size = lax.axis_size(axis)
    return lax.ppermute(value, axis, [(i, (i + step) % size) for i in range(size)])


def swap(value, axis, bit):
    size = lax.axis_size(axis)
    return lax.ppermute(value, axis, [(i, i ^ bit) for i in range(size)])


def pick(index, items):
    return lax.select_n(index, *items)


def slot_onehot(routes, yi, ci, zli, xi, n_y, n_x, tok, top, cap):
    blocks = routes.reshape(n_y, 2, 2, tok, top)
    own = lax.dynamic_index_in_dim(blocks, yi, 0, keepdims=False)
    own = lax.dynamic_index_in_dim(own, ci, 1, keepdims=False)
    experts = zli * n_x + (xi + jnp.arange(n_x, dtype=jnp.int32)) % n_x
    named = jnp.any(own[:, None, :, :] == experts[None, :, None, None], axis=3)
    row = lax.broadcasted_iota(jnp.int32, (tok, tok), 0)
    col = lax.broadcasted_iota(jnp.int32, (tok, tok), 1)
    earlier = (row < col).astype(BF)
    rank = lax.dot_general(
        named.astype(BF), earlier, (((2,), (0,)), ((), ())), preferred_element_type=F32
    )
    rank = jnp.where(named, rank, -1.0)
    slots = lax.broadcasted_iota(jnp.int32, (1, 1, cap, 1), 2).astype(F32)
    return (rank[:, :, None, :] == slots).astype(BF)


def body(tokens, routes, gate_weight, up_weight, hidden_grad, clip_limit):
    n_y, n_x, n_zl = lax.axis_size("y"), lax.axis_size("x"), lax.axis_size("zl")
    n_dp = n_y * 4
    yi, ci = lax.axis_index("y"), lax.axis_index("core")
    zli, xi = lax.axis_index("zl"), lax.axis_index("x")
    tok, feat = tokens.shape
    top = routes.shape[1]
    width, units = gate_weight.shape[1:]
    cap = hidden_grad.shape[2]
    part = n_zl * feat
    rows = 2 * cap

    along_z = lax.all_gather(tokens.T, ("zh", "zl"), axis=0, tiled=True)
    along_z = along_z.reshape(2, part, tok)

    onehot = slot_onehot(routes, yi, ci, zli, xi, n_y, n_x, tok, top, cap)

    def permuted(weight):
        return weight[0].reshape(n_zl, n_x, feat, units).transpose(1, 0, 2, 3).reshape(width, units)

    weights = jnp.concatenate([permuted(gate_weight), permuted(up_weight)], axis=1)

    outgoing = lax.dot_general(
        onehot.reshape(2, n_x * cap, tok),
        along_z,
        (((2,), (2,)), ((0,), (0,))),
        preferred_element_type=F32,
    ).astype(BF).reshape(2, n_x, cap, part)
    arrived = []
    for k in range(n_x):
        piece = outgoing[:, k].reshape(rows, part)
        arrived.append(piece if k == 0 else shift(piece, "x", k))
    own = jnp.concatenate(
        [pick((xi - j) % n_x, arrived) for j in range(n_x)], axis=1
    )

    half = cap
    a = {0: own}
    a[1] = shift(own, "y", 1)
    a[3] = shift(own, "y", -1)
    a[2] = jnp.concatenate(
        [shift(a[1][:half], "y", 1), shift(a[3][half:], "y", -1)], axis=0
    )
    c = {r: swap(a[r], "core", 1) for r in (0, 1, 3, 2)}

    grads = hidden_grad[0].reshape(n_y, 2, 2, cap, units).transpose(0, 2, 1, 3, 4)

    def math(x_rows, grad_rows):
        pre = jnp.dot(x_rows, weights, preferred_element_type=F32)
        gate_pre, up_pre = pre[:, :units], pre[:, units:]
        sigma = jax.nn.sigmoid(gate_pre)
        hidden = (gate_pre * sigma * up_pre).astype(BF)
        g = grad_rows.astype(F32)
        up_act = (g * gate_pre * sigma).astype(BF)
        gate_act = (g * up_pre * sigma * (1.0 + gate_pre * (1.0 - sigma))).astype(BF)
        act = jnp.concatenate([gate_act, up_act], axis=1)
        partial = lax.dot_general(
            act, weights, (((1,), (1,)), ((), ())), preferred_element_type=F32
        )
        return hidden, act, partial

    def grad_rows_of(r):
        g = lax.dynamic_index_in_dim(grads, (yi - r) % n_y, 0, keepdims=False)
        return jnp.where(ci == 0, g, g[::-1]).reshape(2 * rows, units)

    x_list, act_list, hidden_of, summed = [], [], {}, {}
    for group in ((0,), (1, 3), (2,)):
        x_rows = jnp.concatenate([v for r in group for v in (a[r], c[r])], axis=0)
        g_rows = jnp.concatenate([grad_rows_of(r) for r in group], axis=0)
        hid, act, partial = math(x_rows, g_rows)
        x_list.append(x_rows)
        act_list.append(act)
        for n, r in enumerate(group):
            base = n * 2 * rows
            h = hid[base : base + 2 * rows].reshape(2, 2, cap, units)
            hidden_of[r] = jnp.where(ci == 0, h, h[::-1])
            mine = partial[base : base + rows]
            other = partial[base + rows : base + 2 * rows].astype(BF)
            summed[r] = mine + swap(other, "core", 1).astype(F32)

    far = summed[2].astype(BF)
    from_minus = shift(far[:half], "y", 1).astype(F32)
    from_plus = shift(far[half:], "y", -1).astype(F32)
    up_send = jnp.concatenate([summed[3][:half] + from_minus, summed[3][half:]], axis=0)
    down_send = jnp.concatenate([summed[1][:half], summed[1][half:] + from_plus], axis=0)
    up_got = shift(up_send.astype(BF), "y", 1).astype(F32)
    down_got = shift(down_send.astype(BF), "y", -1).astype(F32)
    slot_grad = (summed[0] + up_got + down_got).astype(BF)

    parts = [slot_grad[:, j * part : (j + 1) * part] for j in range(n_x)]
    back = []
    for k in range(n_x):
        piece = pick((xi + k) % n_x, parts)
        piece = piece if k == 0 else shift(piece, "x", k)
        back.append(piece.reshape(2, 1, cap, part))
    back = jnp.concatenate([back[(-k) % n_x] for k in range(n_x)], axis=1)
    token_sum = lax.dot_general(
        back.reshape(2, n_x * cap, part),
        onehot.reshape(2, n_x * cap, tok),
        (((1,), (1,)), ((0,), (0,))),
        preferred_element_type=F32,
    )
    token_grad = lax.psum_scatter(
        token_sum.astype(BF).reshape(2 * part, tok), ("zh", "zl"), scatter_dimension=0, tiled=True
    ).T

    x_all = jnp.concatenate(x_list, axis=0)
    act_all = jnp.concatenate(act_list, axis=0)
    raw = lax.dot_general(x_all, act_all, (((0,), (0,)), ((), ())), preferred_element_type=F32)
    total = jnp.sum(raw * raw).reshape(1)
    total = total + swap(total, "core", 1)
    total = total + swap(total, "y", 1)
    total = total + swap(total, "y", 2)
    total = total + swap(total, "zh", 1)
    root_mean = jnp.sqrt(total / (2.0 * width * units * n_dp) + 1e-06)
    clip_scale = jnp.minimum(1.0, clip_limit / root_mean)
    scaled = (clip_scale[:, None] * raw).astype(BF)

    def restored(value):
        return value.reshape(n_x, n_zl, feat, units).transpose(1, 0, 2, 3).reshape(1, width, units)

    hidden = jnp.stack(
        [pick((yi - j) % n_y, [hidden_of[r] for r in range(n_y)]) for j in range(n_y)]
    )
    hidden = hidden.transpose(0, 2, 1, 3, 4).reshape(1, n_dp, cap, units)
    return (hidden, restored(scaled[:, :units]), restored(scaled[:, units:]), token_grad)


def physical(mesh):
    experts = mesh.shape["expert"]
    devices = mesh.devices.reshape(mesh.shape["dp"] // 4, 2, 2, experts // 4, 4)
    return Mesh(devices, ("y", "zh", "core", "zl", "x"))


def solution(mesh):
    dp, expert = ("y", "zh", "core"), ("zl", "x")
    return jax.shard_map(
        body,
        mesh=physical(mesh),
        in_specs=(
            P(dp, expert),
            P(),
            P(expert, None, dp),
            P(expert, None, dp),
            P(expert, None, None, dp),
            P(expert),
        ),
        out_specs=(
            P(expert, None, None, dp),
            P(expert, None, dp),
            P(expert, None, dp),
            P(dp, expert),
        ),
        check_vma=False,
    )
```

```python
import jax
import jax.numpy as jnp
from jax import lax
from jax.sharding import Mesh, PartitionSpec as P


BF = jnp.bfloat16
F32 = jnp.float32


def shift(value, axis, step):
    size = lax.axis_size(axis)
    return lax.ppermute(value, axis, [(i, (i + step) % size) for i in range(size)])


def swap(value, axis, bit):
    size = lax.axis_size(axis)
    return lax.ppermute(value, axis, [(i, i ^ bit) for i in range(size)])


def pick(index, items):
    return lax.select_n(index, *items)


def slot_onehot(routes, yi, ci, zli, n_y, n_x, tok, top, cap):
    blocks = routes.reshape(n_y, 2, 2, tok, top)
    own = lax.dynamic_index_in_dim(blocks, yi, 0, keepdims=False)
    own = lax.dynamic_index_in_dim(own, ci, 1, keepdims=False)
    experts = zli * n_x + jnp.arange(n_x, dtype=jnp.int32)
    named = jnp.any(own[:, None, :, :] == experts[None, :, None, None], axis=3)
    row = lax.broadcasted_iota(jnp.int32, (tok, tok), 0)
    col = lax.broadcasted_iota(jnp.int32, (tok, tok), 1)
    earlier = (row < col).astype(BF)
    rank = lax.dot_general(
        named.astype(BF), earlier, (((2,), (0,)), ((), ())), preferred_element_type=F32
    )
    rank = jnp.where(named, rank, -1.0)
    slots = lax.broadcasted_iota(jnp.int32, (1, 1, cap, 1), 2).astype(F32)
    return (rank[:, :, None, :] == slots).astype(BF)


def body(tokens, routes, gate_weight, up_weight, hidden_grad, clip_limit):
    n_y, n_x, n_zl = lax.axis_size("y"), lax.axis_size("x"), lax.axis_size("zl")
    n_dp, n_z = n_y * 4, 2 * n_zl
    yi, ci, zli = lax.axis_index("y"), lax.axis_index("core"), lax.axis_index("zl")
    tok, feat = tokens.shape
    top = routes.shape[1]
    width, units = gate_weight.shape[1:]
    cap = hidden_grad.shape[2]
    part = n_zl * feat
    rows = 2 * cap

    along_z = lax.all_gather(tokens.T, ("zh", "zl"), axis=0, tiled=True)
    along_z = along_z.reshape(2, part, tok)

    onehot = slot_onehot(routes, yi, ci, zli, n_y, n_x, tok, top, cap)
    onehot = onehot.reshape(2, n_x * cap, tok)

    def permuted(weight):
        return weight[0].reshape(n_zl, n_x, feat, units).transpose(1, 0, 2, 3).reshape(width, units)

    weights = jnp.concatenate([permuted(gate_weight), permuted(up_weight)], axis=1)

    outgoing = lax.dot_general(
        onehot, along_z, (((2,), (2,)), ((0,), (0,))), preferred_element_type=F32
    ).astype(BF)
    outgoing = outgoing.reshape(2, n_x, cap, part).transpose(1, 0, 2, 3).reshape(n_x, rows, part)
    arrived = lax.all_to_all(outgoing, "x", 0, 0, tiled=True)
    own = jnp.concatenate([arrived[j] for j in range(n_x)], axis=1)

    a1, a3, a2 = shift(own, "y", 1), shift(own, "y", -1), shift(own, "y", 2)
    a_of = {(0,): own, (1, 3): jnp.concatenate([a1, a3], axis=0), (2,): a2}

    grads = hidden_grad[0].reshape(n_y, 2, 2, cap, units).transpose(0, 2, 1, 3, 4)

    def math(x_rows, grad_rows):
        pre = jnp.dot(x_rows, weights, preferred_element_type=F32)
        gate_pre, up_pre = pre[:, :units], pre[:, units:]
        sigma = jax.nn.sigmoid(gate_pre)
        hidden = (gate_pre * sigma * up_pre).astype(BF)
        g = grad_rows.astype(F32)
        up_act = (g * gate_pre * sigma).astype(BF)
        gate_act = (g * up_pre * sigma * (1.0 + gate_pre * (1.0 - sigma))).astype(BF)
        act = jnp.concatenate([gate_act, up_act], axis=1)
        partial = lax.dot_general(
            act, weights, (((1,), (1,)), ((), ())), preferred_element_type=F32
        )
        return hidden, act, partial

    def grad_rows_of(group):
        picked = [lax.dynamic_index_in_dim(grads, (yi - r) % n_y, 0) for r in group]
        both = jnp.concatenate(picked, axis=0).transpose(1, 0, 2, 3, 4)
        return jnp.where(ci == 0, both, both[::-1]).reshape(-1, units)

    x_list, act_list, hidden_of, summed = [], [], {}, {}
    for group in ((0,), (1, 3), (2,)):
        count = len(group) * rows
        x_rows = jnp.concatenate([a_of[group], swap(a_of[group], "core", 1)], axis=0)
        hid, act, partial = math(x_rows, grad_rows_of(group))
        x_list.append(x_rows)
        act_list.append(act)
        both = partial[:count] + swap(partial[count:].astype(BF), "core", 1).astype(F32)
        hid = hid.reshape(2, len(group), 2, cap, units)
        hid = jnp.where(ci == 0, hid, hid[::-1])
        for n, r in enumerate(group):
            hidden_of[r] = hid[:, n]
            summed[r] = both[n * rows : (n + 1) * rows]

    got = [shift(summed[r].astype(BF), "y", -r).astype(F32) for r in (1, 3, 2)]
    slot_grad = (summed[0] + got[0] + got[1] + got[2]).astype(BF)

    back = jnp.stack([slot_grad[:, j * part : (j + 1) * part] for j in range(n_x)])
    back = lax.all_to_all(back, "x", 0, 0, tiled=True)
    back = back.reshape(n_x, 2, cap, part).transpose(1, 0, 2, 3).reshape(2, n_x * cap, part)
    token_sum = lax.dot_general(
        back, onehot, (((1,), (1,)), ((0,), (0,))), preferred_element_type=F32
    ).reshape(n_z, feat, tok)

    x_all = jnp.concatenate(x_list, axis=0)
    act_all = jnp.concatenate(act_list, axis=0)
    raw = lax.dot_general(x_all, act_all, (((0,), (0,)), ((), ())), preferred_element_type=F32)
    total = jnp.sum(raw * raw).reshape(1)
    total = total + swap(total, "core", 1)
    total = total + swap(total, "y", 1)
    total = total + swap(total, "y", 2)

    sent, total = lax.optimization_barrier((token_sum.astype(BF), total))
    landed = lax.all_to_all(sent, ("zh", "zl"), 0, 0, tiled=True)
    token_grad = jnp.sum(landed.astype(F32), axis=0).astype(BF).T
    other_half = swap(total, "zh", 1)
    total = total + other_half
    root_mean = jnp.sqrt(total / (2.0 * width * units * n_dp) + 1e-06)
    clip_scale = jnp.minimum(1.0, clip_limit / root_mean)
    scaled = (clip_scale[:, None] * raw).astype(BF)

    def restored(value):
        return value.reshape(n_x, n_zl, feat, units).transpose(1, 0, 2, 3).reshape(1, width, units)

    hidden = jnp.stack(
        [pick((yi - j) % n_y, [hidden_of[r] for r in range(n_y)]) for j in range(n_y)]
    )
    hidden = hidden.transpose(0, 2, 1, 3, 4).reshape(1, n_dp, cap, units)
    return (hidden, restored(scaled[:, :units]), restored(scaled[:, units:]), token_grad)


def physical(mesh):
    experts = mesh.shape["expert"]
    devices = mesh.devices.reshape(mesh.shape["dp"] // 4, 2, 2, experts // 4, 4)
    return Mesh(devices, ("y", "zh", "core", "zl", "x"))


def solution(mesh):
    dp, expert = ("y", "zh", "core"), ("zl", "x")
    return jax.shard_map(
        body,
        mesh=physical(mesh),
        in_specs=(
            P(dp, expert),
            P(),
            P(expert, None, dp),
            P(expert, None, dp),
            P(expert, None, None, dp),
            P(expert),
        ),
        out_specs=(
            P(expert, None, None, dp),
            P(expert, None, dp),
            P(expert, None, dp),
            P(dp, expert),
        ),
        check_vma=False,
    )
```

```python
import jax
import jax.numpy as jnp
from jax import lax
from jax.sharding import Mesh, PartitionSpec as P


BF = jnp.bfloat16
F32 = jnp.float32


def shift(value, axis, step):
    size = lax.axis_size(axis)
    return lax.ppermute(value, axis, [(i, (i + step) % size) for i in range(size)])


def swap(value, axis, bit):
    size = lax.axis_size(axis)
    return lax.ppermute(value, axis, [(i, i ^ bit) for i in range(size)])


def pick(index, items):
    return lax.select_n(index, *items)


def slot_onehot(routes, yi, ci, zli, n_y, n_x, tok, top, cap):
    blocks = routes.reshape(n_y, 2, 2, tok, top)
    own = lax.dynamic_index_in_dim(blocks, yi, 0, keepdims=False)
    own = lax.dynamic_index_in_dim(own, ci, 1, keepdims=False)
    experts = zli * n_x + jnp.arange(n_x, dtype=jnp.int32)
    chosen = jnp.any(own[:, None, :, :] == experts[None, :, None, None], axis=3)
    row = lax.broadcasted_iota(jnp.int32, (tok, tok), 0)
    col = lax.broadcasted_iota(jnp.int32, (tok, tok), 1)
    earlier = (row < col).astype(BF)
    rank = lax.dot_general(
        chosen.astype(BF), earlier, (((2,), (0,)), ((), ())), preferred_element_type=F32
    )
    rank = jnp.where(chosen, rank, -1.0)
    slots = lax.broadcasted_iota(jnp.int32, (1, 1, cap, 1), 2).astype(F32)
    return (rank[:, :, None, :] == slots).astype(BF)


def body(tokens, routes, gate_weight, up_weight, hidden_grad, clip_limit):
    n_y, n_x, n_zl = lax.axis_size("y"), lax.axis_size("x"), lax.axis_size("zl")
    n_dp, n_z = n_y * 4, 2 * n_zl
    yi, ci, zli = lax.axis_index("y"), lax.axis_index("core"), lax.axis_index("zl")
    tok, feat = tokens.shape
    top = routes.shape[1]
    width, units = gate_weight.shape[1:]
    cap = hidden_grad.shape[2]
    part = n_zl * feat
    rows = 2 * cap

    along_z = lax.all_gather(tokens.T, ("zh", "zl"), axis=0, tiled=True)
    along_z = along_z.reshape(2, part, tok)

    onehot = slot_onehot(routes, yi, ci, zli, n_y, n_x, tok, top, cap)
    onehot = onehot.reshape(2, n_x * cap, tok)

    def permuted(weight):
        return weight[0].reshape(n_zl, n_x, feat, units).transpose(1, 0, 2, 3).reshape(width, units)

    weights = jnp.concatenate([permuted(gate_weight), permuted(up_weight)], axis=1)

    outgoing = lax.dot_general(
        onehot, along_z, (((2,), (2,)), ((0,), (0,))), preferred_element_type=F32
    ).astype(BF)
    outgoing = outgoing.reshape(2, n_x, cap, part).transpose(1, 0, 2, 3).reshape(n_x, rows, part)
    arrived = lax.all_to_all(outgoing, "x", 0, 0, tiled=True)
    own = jnp.concatenate([arrived[j] for j in range(n_x)], axis=1)

    a2 = shift(own, "y", 2)
    a1 = shift(own, "y", 1)
    a3 = shift(own, "y", -1)
    a_of = {(0,): own, (1, 3, 2): jnp.concatenate([a1, a3, a2], axis=0)}

    grads = hidden_grad[0].reshape(n_y, 2, 2, cap, units).transpose(0, 2, 1, 3, 4)

    def math(x_rows, grad_rows):
        pre = jnp.dot(x_rows, weights, preferred_element_type=F32)
        gate_pre, up_pre = pre[:, :units], pre[:, units:]
        sigma = jax.nn.sigmoid(gate_pre)
        hidden = (gate_pre * sigma * up_pre).astype(BF)
        g = grad_rows.astype(F32)
        up_act = (g * gate_pre * sigma).astype(BF)
        gate_act = (g * up_pre * sigma * (1.0 + gate_pre * (1.0 - sigma))).astype(BF)
        act = jnp.concatenate([gate_act, up_act], axis=1)
        partial = lax.dot_general(
            act, weights, (((1,), (1,)), ((), ())), preferred_element_type=F32
        )
        return hidden, act, partial

    def grad_rows_of(group):
        picked = [lax.dynamic_index_in_dim(grads, (yi - r) % n_y, 0) for r in group]
        both = jnp.concatenate(picked, axis=0).transpose(1, 0, 2, 3, 4)
        return jnp.where(ci == 0, both, both[::-1]).reshape(-1, units)

    x_list, act_list, hidden_of, summed = [], [], {}, {}
    for group in ((0,), (1, 3, 2)):
        count = len(group) * rows
        twin = swap(a_of[group], "core", 1)
        x_rows = jnp.concatenate([a_of[group], twin], axis=0)
        hid, act, partial = math(x_rows, grad_rows_of(group))
        x_list.append(x_rows)
        act_list.append(act)
        both = partial[:count] + swap(partial[count:].astype(BF), "core", 1).astype(F32)
        hid = hid.reshape(2, len(group), 2, cap, units)
        hid = jnp.where(ci == 0, hid, hid[::-1])
        for n, r in enumerate(group):
            hidden_of[r] = hid[:, n]
            summed[r] = both[n * rows : (n + 1) * rows]

    got = []
    for r in (1, 3, 2):
        got.append(shift(summed[r].astype(BF), "y", -r).astype(F32))

    x_all = jnp.concatenate(x_list, axis=0)
    act_all = jnp.concatenate(act_list, axis=0)
    raw = lax.dot_general(x_all, act_all, (((0,), (0,)), ((), ())), preferred_element_type=F32)
    total = jnp.sum(raw * raw).reshape(1)
    other_half = swap(total, "zh", 1)
    total = total + other_half
    total = total + swap(total, "core", 1)

    base, total = lax.optimization_barrier((summed[0], total))
    slot_grad = (base + got[0] + got[1] + got[2]).astype(BF)

    back = jnp.stack([slot_grad[:, j * part : (j + 1) * part] for j in range(n_x)])
    back = lax.all_to_all(back, "x", 0, 0, tiled=True)
    back = back.reshape(n_x, 2, cap, part).transpose(1, 0, 2, 3).reshape(2, n_x * cap, part)
    token_sum = lax.dot_general(
        back, onehot, (((1,), (1,)), ((0,), (0,))), preferred_element_type=F32
    ).reshape(n_z, feat, tok)

    sent, total = lax.optimization_barrier((token_sum.astype(BF), total))
    landed = lax.all_to_all(sent, ("zh", "zl"), 0, 0, tiled=True)
    token_grad = jnp.sum(landed.astype(F32), axis=0).astype(BF).T
    other = swap(total, "y", 1)
    total = total + other
    total = total + swap(total, "y", 2)
    root_mean = jnp.sqrt(total / (2.0 * width * units * n_dp) + 1e-06)
    clip_scale = jnp.minimum(1.0, clip_limit / root_mean)
    scaled = (clip_scale[:, None] * raw).astype(BF)

    def restored(value):
        return value.reshape(n_x, n_zl, feat, units).transpose(1, 0, 2, 3).reshape(1, width, units)

    hidden = jnp.stack(
        [pick((yi - j) % n_y, [hidden_of[r] for r in range(n_y)]) for j in range(n_y)]
    )
    hidden = hidden.transpose(0, 2, 1, 3, 4).reshape(1, n_dp, cap, units)
    return (hidden, restored(scaled[:, :units]), restored(scaled[:, units:]), token_grad)


def physical(mesh):
    experts = mesh.shape["expert"]
    devices = mesh.devices.reshape(mesh.shape["dp"] // 4, 2, 2, experts // 4, 4)
    return Mesh(devices, ("y", "zh", "core", "zl", "x"))


def solution(mesh):
    dp, expert = ("y", "zh", "core"), ("zl", "x")
    return jax.shard_map(
        body,
        mesh=physical(mesh),
        in_specs=(
            P(dp, expert),
            P(),
            P(expert, None, dp),
            P(expert, None, dp),
            P(expert, None, None, dp),
            P(expert),
        ),
        out_specs=(
            P(expert, None, None, dp),
            P(expert, None, dp),
            P(expert, None, dp),
            P(dp, expert),
        ),
        check_vma=False,
    )
```

```python
import jax
import jax.numpy as jnp
from jax import lax
from jax.sharding import Mesh, PartitionSpec as P


BF = jnp.bfloat16
F32 = jnp.float32


def shift(value, axis, step):
    size = lax.axis_size(axis)
    return lax.ppermute(value, axis, [(i, (i + step) % size) for i in range(size)])


def swap(value, axis, bit):
    size = lax.axis_size(axis)
    return lax.ppermute(value, axis, [(i, i ^ bit) for i in range(size)])


def pick(index, items):
    return lax.select_n(index, *items)


def slot_onehot(routes, yi, ci, zli, n_y, n_x, tok, top, cap):
    blocks = routes.reshape(n_y, 2, 2, tok, top)
    own = lax.dynamic_index_in_dim(blocks, yi, 0, keepdims=False)
    own = lax.dynamic_index_in_dim(own, ci, 1, keepdims=False)
    experts = zli * n_x + jnp.arange(n_x, dtype=jnp.int32)
    chosen = jnp.any(own[:, None, :, :] == experts[None, :, None, None], axis=3)
    row = lax.broadcasted_iota(jnp.int32, (tok, tok), 0)
    col = lax.broadcasted_iota(jnp.int32, (tok, tok), 1)
    earlier = (row < col).astype(BF)
    rank = lax.dot_general(
        chosen.astype(BF), earlier, (((2,), (0,)), ((), ())), preferred_element_type=F32
    )
    rank = jnp.where(chosen, rank, -1.0)
    slots = lax.broadcasted_iota(jnp.int32, (1, 1, cap, 1), 2).astype(F32)
    return (rank[:, :, None, :] == slots).astype(BF)


def body(tokens, routes, gate_weight, up_weight, hidden_grad, clip_limit):
    n_y, n_x, n_zl = lax.axis_size("y"), lax.axis_size("x"), lax.axis_size("zl")
    n_dp, n_z = n_y * 4, 2 * n_zl
    yi, ci, zli = lax.axis_index("y"), lax.axis_index("core"), lax.axis_index("zl")
    tok, feat = tokens.shape
    top = routes.shape[1]
    width, units = gate_weight.shape[1:]
    cap = hidden_grad.shape[2]
    part = n_zl * feat
    rows = 2 * cap

    along_z = lax.all_gather(tokens.T, ("zh", "zl"), axis=0, tiled=True)
    along_z = along_z.reshape(2, part, tok)

    onehot = slot_onehot(routes, yi, ci, zli, n_y, n_x, tok, top, cap)
    onehot = onehot.reshape(2, n_x * cap, tok)

    def permuted(weight):
        return weight[0].reshape(n_zl, n_x, feat, units).transpose(1, 0, 2, 3).reshape(width, units)

    weights = jnp.concatenate([permuted(gate_weight), permuted(up_weight)], axis=1)

    outgoing = lax.dot_general(
        onehot, along_z, (((2,), (2,)), ((0,), (0,))), preferred_element_type=F32
    ).astype(BF)
    outgoing = outgoing.reshape(2, n_x, cap, part).transpose(1, 0, 2, 3).reshape(n_x, rows, part)
    arrived = lax.all_to_all(outgoing, "x", 0, 0, tiled=True)
    own = jnp.concatenate([arrived[j] for j in range(n_x)], axis=1)

    grads = hidden_grad[0].reshape(n_y, 2, 2, cap, units).transpose(0, 2, 1, 3, 4)

    def grad_rows_of(group):
        picked = [lax.dynamic_index_in_dim(grads, (yi - r) % n_y, 0) for r in group]
        both = jnp.concatenate(picked, axis=0).transpose(1, 0, 2, 3, 4)
        return jnp.where(ci == 0, both, both[::-1]).reshape(-1, units)

    groups = ((0,), (1, 3, 2))
    own, weights, *grad_rows = lax.optimization_barrier(
        (own, weights, *[grad_rows_of(group) for group in groups])
    )

    a2 = shift(own, "y", 2)
    a1 = shift(own, "y", 1)
    a3 = shift(own, "y", -1)
    a_of = {(0,): own, (1, 3, 2): jnp.concatenate([a1, a3, a2], axis=0)}

    def math(x_rows, grad_rows):
        pre = jnp.dot(x_rows, weights, preferred_element_type=F32)
        gate_pre, up_pre = pre[:, :units], pre[:, units:]
        sigma = jax.nn.sigmoid(gate_pre)
        hidden = (gate_pre * sigma * up_pre).astype(BF)
        g = grad_rows.astype(F32)
        up_act = (g * gate_pre * sigma).astype(BF)
        gate_act = (g * up_pre * sigma * (1.0 + gate_pre * (1.0 - sigma))).astype(BF)
        act = jnp.concatenate([gate_act, up_act], axis=1)
        partial = lax.dot_general(
            act, weights, (((1,), (1,)), ((), ())), preferred_element_type=F32
        )
        return hidden, act, partial

    x_list, act_list, hidden_of, summed = [], [], {}, {}
    for number, group in enumerate(groups):
        count = len(group) * rows
        twin = swap(a_of[group], "core", 1)
        x_rows = jnp.concatenate([a_of[group], twin], axis=0)
        hid, act, partial = math(x_rows, grad_rows[number])
        x_list.append(x_rows)
        act_list.append(act)
        other = swap(partial[count:].astype(BF), "core", 1)
        both = partial[:count] + other.astype(F32)
        hid = hid.reshape(2, len(group), 2, cap, units)
        hid = jnp.where(ci == 0, hid, hid[::-1])
        for n, r in enumerate(group):
            hidden_of[r] = hid[:, n]
            summed[r] = both[n * rows : (n + 1) * rows]

    got = []
    for r in (1, 3, 2):
        got.append(shift(summed[r].astype(BF), "y", -r).astype(F32))

    x_all = jnp.concatenate(x_list, axis=0)
    act_all = jnp.concatenate(act_list, axis=0)
    raw = lax.dot_general(x_all, act_all, (((0,), (0,)), ((), ())), preferred_element_type=F32)
    total = jnp.sum(raw * raw).reshape(1)
    base, total = lax.optimization_barrier((summed[0], total))
    other_half = swap(total, "zh", 1)
    slot_grad = (base + got[0] + got[1] + got[2]).astype(BF)

    back = jnp.stack([slot_grad[:, j * part : (j + 1) * part] for j in range(n_x)])
    back = lax.all_to_all(back, "x", 0, 0, tiled=True)
    back = back.reshape(n_x, 2, cap, part).transpose(1, 0, 2, 3).reshape(2, n_x * cap, part)
    token_sum = lax.dot_general(
        back, onehot, (((1,), (1,)), ((0,), (0,))), preferred_element_type=F32
    ).reshape(n_z, feat, tok)

    sent, total = lax.optimization_barrier((token_sum.astype(BF), total + other_half))
    landed = lax.all_to_all(sent, ("zh", "zl"), 0, 0, tiled=True)
    token_grad = jnp.sum(landed.astype(F32), axis=0).astype(BF).T
    other = swap(total, "core", 1)
    total = total + other
    total = total + swap(total, "y", 1)
    total = total + swap(total, "y", 2)
    root_mean = jnp.sqrt(total / (2.0 * width * units * n_dp) + 1e-06)
    clip_scale = jnp.minimum(1.0, clip_limit / root_mean)
    scaled = (clip_scale[:, None] * raw).astype(BF)

    def restored(value):
        return value.reshape(n_x, n_zl, feat, units).transpose(1, 0, 2, 3).reshape(1, width, units)

    hidden = jnp.stack(
        [pick((yi - j) % n_y, [hidden_of[r] for r in range(n_y)]) for j in range(n_y)]
    )
    hidden = hidden.transpose(0, 2, 1, 3, 4).reshape(1, n_dp, cap, units)
    return (hidden, restored(scaled[:, :units]), restored(scaled[:, units:]), token_grad)


def physical(mesh):
    experts = mesh.shape["expert"]
    devices = mesh.devices.reshape(mesh.shape["dp"] // 4, 2, 2, experts // 4, 4)
    return Mesh(devices, ("y", "zh", "core", "zl", "x"))


def solution(mesh):
    dp, expert = ("y", "zh", "core"), ("zl", "x")
    return jax.shard_map(
        body,
        mesh=physical(mesh),
        in_specs=(
            P(dp, expert),
            P(),
            P(expert, None, dp),
            P(expert, None, dp),
            P(expert, None, None, dp),
            P(expert),
        ),
        out_specs=(
            P(expert, None, None, dp),
            P(expert, None, dp),
            P(expert, None, dp),
            P(dp, expert),
        ),
        check_vma=False,
    )
```
